32 devices in a mesh: orb: 4 (over z), box: 8 (over y, x, core).
Axes of the slice: x: 2, y: 2, z: 4, core: 2. Of those that a mesh axis runs over, the one named last changes fastest.
Arguments:
- coarse: bfloat16 [4, 8, 729, 1024], P('orb', None, None, 'box'), may hold values from -1.5 to 1.5
- wavelets: bfloat16 [4, 7, 729, 1024], P('orb', None, None, 'box'), may hold values from -1.5 to 1.5
- leaf_flags: int32 [4, 1024], P('orb', 'box'), may hold values 0 or 1
- child_key1: int32 [1024], P('box'), may hold values from 0 to 8191, as said below
- child_key2: int32 [2048], P('box'), may hold values from 0 to 8191, as said below
- counts: int32 [8], P('box'), may hold values from 128 to 256, as said below
Outputs:
- density: float32 [729, 2048], P(None, 'box')
The draws below stay inside these ranges and needn't reach their ends.
Inputs may be any that keep to these rules, and one draw needn't show every extreme that they name: `child_key1`: within each curve range of 128 entries the keys rise and name distinct children; each parent lies in the same range or among the last 32 boxes of the range before; every range but the first has an entry naming a child of the first of those 32 boxes. `child_key2`: within each curve range of 256 entries the keys rise and name distinct children; each parent lies in the same range or among the last 32 boxes of the range before; every range but the first has an entry naming a child of the first of those 32 boxes. `counts`: some range is full in every draw and some range holds the fewest.
All inputs are finite; a program needn't handle non-finite values. No bound on the sum of `leaf_flags` on one device may be relied on, other than what follows from the above.
Results may differ from the reference program's by a relative error of at most 0.0003.
Values may be sent and summed in bfloat16 or wider, within the bound.
A program may use at most 64 MiB of HBM per device.

```python
import math
import jax
import jax.numpy as jnp
import numpy as np
from jax import lax

BOX_DEV = 128
ORBITALS = 4
BOXES = 1024
LEAVES = 2048
SPILL = 32


def range_keys(key, slots):
    ranges = BOXES // BOX_DEV
    margin = 8 * SPILL
    choices_all = 8 * (BOX_DEV + SPILL)
    choices_first = 8 * BOX_DEV

    def one_range(position):
        folded = jax.random.fold_in(key, position)
        key_rest, key_first = jax.random.split(folded)
        middle = 1 + jax.random.permutation(key_rest, choices_all - 2)[:slots - 2]
        picked = jnp.concatenate([jnp.zeros((1,), jnp.int32), middle.astype(jnp.int32), jnp.full((1,), choices_all - 1, jnp.int32)])
        earlier = picked < margin
        shifted = picked - margin
        parent = jnp.where(earlier, (position - 1) * BOX_DEV + BOX_DEV - SPILL + picked // 8, position * BOX_DEV + shifted // 8)
        octant = jnp.where(earlier, picked % 8, shifted % 8)
        general = 8 * parent + octant
        middle_first = 1 + jax.random.permutation(key_first, choices_first - 2)[:slots - 2]
        first_codes = jnp.concatenate([jnp.zeros((1,), jnp.int32), middle_first.astype(jnp.int32), jnp.full((1,), choices_first - 1, jnp.int32)])
        codes = jnp.where(position == 0, first_codes, general)
        return jnp.sort(codes)
    return jax.vmap(one_range)(jnp.arange(ranges, dtype=jnp.int32)).reshape(-1).astype(jnp.int32)


def draw_child_key1(key, part):
    return range_keys(jax.random.fold_in(key, 11), BOX_DEV)


def draw_child_key2(key, part):
    return range_keys(jax.random.fold_in(key, 23), 2 * BOX_DEV)


def draw_counts(key, part):
    ranges = BOXES // BOX_DEV
    key_all, key_full, key_low = jax.random.split(jax.random.fold_in(key, 37), 3)
    values = jax.random.randint(key_all, (ranges,), BOX_DEV, 2 * BOX_DEV + 1, dtype=jnp.int32)
    fullest = jax.random.randint(key_full, (), 0, ranges, dtype=jnp.int32)
    lowest = (fullest + 1 + jax.random.randint(key_low, (), 0, ranges - 1, dtype=jnp.int32)) % ranges
    positions = jnp.arange(ranges, dtype=jnp.int32)
    values = jnp.where(positions == fullest, 2 * BOX_DEV, values)
    values = jnp.where(positions == lowest, BOX_DEV, values)
    return values.astype(jnp.int32)


def place_ends(values, stream_key, least, top_value):
    index_at = [jax.random.randint(jax.random.fold_in(stream_key, axis), (), 0, length) for axis, length in enumerate(values.shape)]
    widest = values.shape.index(max(values.shape))
    next_to = index_at[:widest] + [(index_at[widest] + 1) % values.shape[widest]] + index_at[widest + 1:]
    return values.at[tuple(index_at)].set(least).at[tuple(next_to)].set(top_value)


def levels(rng, shape, pieces, low, largest):
    loudness, own = 1.0, jax.random.fold_in(rng, 6)
    for dim, parts in pieces:
        draws = jnp.exp(jax.random.uniform(jax.random.fold_in(own, dim), (parts,), jnp.float32, low / len(pieces), largest / len(pieces)))
        loudness = loudness * jnp.repeat(draws, shape[dim] // parts).reshape([-1 if axis == dim else 1 for axis in range(len(shape))])
    return loudness


def normal_values(key, dims, scale, reach, pieces=(), kind=jnp.bfloat16):
    values = jax.random.normal(key, dims, jnp.float32) * scale
    if len(pieces) > 0:
        values = levels(key, dims, pieces, -0.22, 0.18) * values
    return jnp.clip(values, min=-reach, max=reach).astype(kind)


def setup_inputs(seed: int = 0) -> dict:
    splits = jax.random.split(jax.random.key(seed), 7)
    return {
        "coarse": normal_values(splits[0], (ORBITALS, 8, 729, BOXES), 0.25, 1.5, ((0, 4), (3, 8))),
        "wavelets": normal_values(splits[1], (ORBITALS, 7, 729, BOXES), 0.25, 1.5, ((0, 4), (3, 8))),
        "leaf_flags": place_ends((jax.random.randint(splits[2], (ORBITALS, BOXES), 0, 2) < 1).astype(jnp.int32), jax.random.fold_in(splits[2], 1), 0, 1),
        "child_key1": draw_child_key1(jax.random.fold_in(splits[6], 71), 0),
        "child_key2": draw_child_key2(jax.random.fold_in(splits[6], 71), 0),
        "counts": draw_counts(jax.random.fold_in(splits[6], 71), 0),
    }


def legendre_pair(order, where):
    before = where * 0.0 + 1.0
    value = where
    for degree in range(1, order):
        before, value = (value, ((2 * degree + 1) * where * value - degree * before) / (degree + 1))
    return (value, before)

def gauss_rule(order):
    nodes = np.cos(np.pi * (np.arange(order) + 0.75) / (order + 0.5))
    for repeat in range(40):
        value, before = legendre_pair(order, nodes)
        slope = order * (nodes * value - before) / (nodes * nodes - 1.0)
        nodes = nodes - value / slope
    value, before = legendre_pair(order, nodes)
    slope = order * (nodes * value - before) / (nodes * nodes - 1.0)
    weights = 2.0 / ((1.0 - nodes * nodes) * slope * slope)
    return (nodes[::-1], weights[::-1])

def legendre_basis(where):
    shifted = 2.0 * where - 1.0
    rows = [shifted * 0.0 + 1.0, shifted]
    for degree in range(1, 8):
        rows.append(((2 * degree + 1) * shifted * rows[degree] - degree * rows[degree - 1]) / (degree + 1))
    scale = np.sqrt(2.0 * np.arange(9) + 1.0)[:, None]
    return np.stack(rows, 0) * scale

def complement_rows(scaling_rows):
    members = [scaling_rows[index] for index in range(9)]
    kept = []
    identity = np.eye(18)
    for column in range(18):
        vector = identity[column]
        for passes in range(2):
            for member in members + kept:
                vector = vector - np.dot(member, vector) * member
        length = np.sqrt(np.dot(vector, vector))
        if length > 0.1 and len(kept) < 9:
            kept.append(vector / length)
    return np.stack(kept, 0)

def wavelet_tables():
    nodes, weights = gauss_rule(24)
    points = 0.5 * (nodes + 1.0)
    halves = 0.5 * weights
    lower = legendre_basis(0.5 * points) * halves @ legendre_basis(points).T / math.sqrt(2.0)
    upper = legendre_basis(0.5 * points + 0.5) * halves @ legendre_basis(points).T / math.sqrt(2.0)
    scaling_rows = np.concatenate([lower, upper], 1)
    wavelet_rows = complement_rows(scaling_rows)
    matrix = np.concatenate([scaling_rows, wavelet_rows], 0).reshape(2, 9, 2, 9)
    gauss, gauss_weights = gauss_rule(9)
    quad = legendre_basis(0.5 * (gauss + 1.0)).T * np.sqrt(0.5 * gauss_weights)[:, None]
    return (jnp.asarray(matrix, dtype=jnp.float32), jnp.asarray(quad, dtype=jnp.float32))

def expand(blocks, filters):
    highest = lax.Precision.HIGHEST
    cube = blocks.reshape(2, 2, 2, 9, 9, 9, -1)
    cube = jnp.einsum('abcijlz,aiod->bcjlodz', cube, filters, precision=highest)
    cube = jnp.einsum('bcjlodz,bjqe->clodqez', cube, filters, precision=highest)
    cube = jnp.einsum('clodqez,clrf->defoqrz', cube, filters, precision=highest)
    return cube.reshape(729, 8, -1)

def select(children, codes):
    width = children.shape[2]
    flat = children.reshape(729, 8 * width)
    index = (codes % 8 * width + codes // 8).astype(jnp.int32)
    return jnp.take(flat, index, axis=1)

def quadrature(scaling, quad):
    highest = lax.Precision.HIGHEST
    cube = scaling.reshape(9, 9, 9, -1)
    cube = jnp.einsum('ijlz,gi->gjlz', cube, quad, precision=highest)
    cube = jnp.einsum('gjlz,hj->ghlz', cube, quad, precision=highest)
    cube = jnp.einsum('ghlz,kl->ghkz', cube, quad, precision=highest)
    return cube.reshape(729, -1)

def reference(coarse, wavelets, leaf_flags, child_key1, child_key2, counts):
    filters, quad = wavelet_tables()

    def orbital_step(total, items):
        coarse_one, wave_one, leaf_one = items
        children = expand(coarse_one.astype(jnp.float32), filters)
        first = select(children, child_key1)
        keep = (1 - leaf_one).astype(jnp.float32)
        blocks = jnp.concatenate([first[None], wave_one.astype(jnp.float32) * keep], 0)
        children = expand(blocks, filters)
        second = select(children, child_key2)
        values = quadrature(second, quad)
        return (total + values * values, None)
    start = jnp.zeros((729, LEAVES), jnp.float32)
    total, unused = lax.scan(orbital_step, start, (coarse, wavelets, leaf_flags))
    slots = jnp.arange(LEAVES, dtype=jnp.int32)
    live = slots % (2 * BOX_DEV) < counts[slots // (2 * BOX_DEV)]
    return 2.0 * total * live.astype(jnp.float32)
```

```python
import math

import jax
import jax.numpy as jnp
import numpy as np
from jax import lax
from jax.experimental import pallas as pl
from jax.experimental.pallas import tpu as pltpu
from jax.sharding import PartitionSpec as P

SPILL = 32


def legendre_pair(order, where):
    before = where * 0.0 + 1.0
    value = where
    for degree in range(1, order):
        before, value = (value, ((2 * degree + 1) * where * value - degree * before) / (degree + 1))
    return (value, before)


def gauss_rule(order):
    nodes = np.cos(np.pi * (np.arange(order) + 0.75) / (order + 0.5))
    for repeat in range(40):
        value, before = legendre_pair(order, nodes)
        slope = order * (nodes * value - before) / (nodes * nodes - 1.0)
        nodes = nodes - value / slope
    value, before = legendre_pair(order, nodes)
    slope = order * (nodes * value - before) / (nodes * nodes - 1.0)
    weights = 2.0 / ((1.0 - nodes * nodes) * slope * slope)
    return (nodes[::-1], weights[::-1])


def legendre_basis(where):
    shifted = 2.0 * where - 1.0
    rows = [shifted * 0.0 + 1.0, shifted]
    for degree in range(1, 8):
        rows.append(
            ((2 * degree + 1) * shifted * rows[degree] - degree * rows[degree - 1]) / (degree + 1)
        )
    scale = np.sqrt(2.0 * np.arange(9) + 1.0)[:, None]
    return np.stack(rows, 0) * scale


def complement_rows(scaling_rows):
    members = [scaling_rows[index] for index in range(9)]
    kept = []
    identity = np.eye(18)
    for column in range(18):
        vector = identity[column]
        for passes in range(2):
            for member in members + kept:
                vector = vector - np.dot(member, vector) * member
        length = np.sqrt(np.dot(vector, vector))
        if length > 0.1 and len(kept) < 9:
            kept.append(vector / length)
    return np.stack(kept, 0)


def wavelet_tables():
    nodes, weights = gauss_rule(24)
    points = 0.5 * (nodes + 1.0)
    halves = 0.5 * weights
    lower = legendre_basis(0.5 * points) * halves @ legendre_basis(points).T / math.sqrt(2.0)
    upper = legendre_basis(0.5 * points + 0.5) * halves @ legendre_basis(points).T / math.sqrt(2.0)
    scaling_rows = np.concatenate([lower, upper], 1)
    wavelet_rows = complement_rows(scaling_rows)
    matrix = np.concatenate([scaling_rows, wavelet_rows], 0).reshape(2, 9, 2, 9)
    gauss, gauss_weights = gauss_rule(9)
    quad = legendre_basis(0.5 * (gauss + 1.0)).T * np.sqrt(0.5 * gauss_weights)[:, None]
    return (matrix.reshape(18, 2, 9), quad)


ROWS = 729
PADDED = 800
SEGMENT = 92
HALVES = (((0, 1), (2, 3, 4)), ((5, 6), (7, 8), (9, 10)))
GROUPS = ((0, 1), (2, 3), (4, 5), (6, 7), (8, 9, 10))
THIRD_GROUPS = ((0, 1), (2, 3))
QUARTER = 192
PARTS = 3
WIDTH = 27
PIECE = 243
PIECE_ROWS = 256
SCALE_ROW = 248
PART_ROWS = 288
LAG = 2


def local_keys(keys, boxes):
    key = keys - lax.axis_index("box") * (8 * boxes)
    return (lax.shift_right_arithmetic(key, 3), key & 7)


def spread_matrix(boxes, group):
    source = lax.broadcasted_iota(jnp.int32, (boxes, 128), 0)
    target = lax.broadcasted_iota(jnp.int32, (boxes, 128), 1)
    hit = (source - (boxes - SPILL) == target - SPILL * group) & (source >= boxes - SPILL)
    return hit.astype(jnp.float32).astype(jnp.bfloat16)


def pick_own(column, boxes):
    row = lax.broadcasted_iota(jnp.int32, (boxes, column.shape[1]), 0)
    return (row == column).astype(jnp.float32)


def pick_spilled(column, group):
    row = lax.broadcasted_iota(jnp.int32, (128, column.shape[1]), 0)
    hit = (row == column + SPILL * (group + 1)) & (column < 0)
    return hit.astype(jnp.float32)


def fill_coefficients(coef_ref, octant, table):
    for axis in range(3):
        bit = jnp.broadcast_to((octant >> axis) & 1, (8, 128)) == 1
        for k in range(18):
            for f in range(9):
                coef_ref[axis * 162 + k * 9 + f] = jnp.where(
                    bit, np.float32(table[k, 1, f]), np.float32(table[k, 0, f])
                )


def contract(source_ref, low, high, coef_ref, axis, store, groups=GROUPS, first=0, outputs=9, width=81):
    def load(block, row):
        if len(source_ref.shape) == 2:
            return source_ref[pl.ds(8 * row + block, 8, stride=72), :]
        return source_ref[block, pl.ds(row, 8, stride=9), :]

    for group in groups:
        inputs = [[load(block, l + 72 * t) for block in (low, high) for l in range(9)] for t in group]
        for f in range(outputs):
            sums = [None] * len(group)
            for k in range(18):
                weight = coef_ref[axis * 162 + k * 9 + first + f]
                for n in range(len(group)):
                    term = weight * inputs[n][k]
                    sums[n] = term if sums[n] is None else sums[n] + term
            for n, t in enumerate(group):
                store(width * f + 8 * t, min(8, width - 8 * t), sums[n])


def lower_axis(source_ref, target_ref, coef_ref, axis, start, stop, groups=GROUPS, **kinds):
    def step(index, carry):
        def store(row, count, value):
            target_ref[index, row : row + count, :] = value[:count]

        contract(source_ref, 2 * index, 2 * index + 1, coef_ref, axis, store, groups, **kinds)
        return carry

    lax.fori_loop(start, stop, step, 0)


def dot(left, right):
    return jnp.dot(left, right, preferred_element_type=jnp.float32)


def scale_of(steps):
    return jnp.exp2(steps * np.float32(1.0 / 256.0))


def encode(value):
    top = jnp.maximum(jnp.max(jnp.abs(value), axis=0, keepdims=True), 1e-30)
    steps = jnp.ceil(jnp.log2(top) * 256.0)
    code = jnp.round(value[:SCALE_ROW] * (32700.0 / scale_of(steps)))
    code = jnp.concatenate([code, jnp.broadcast_to(steps, (PIECE_ROWS - SCALE_ROW, 128))], 0)
    return code.astype(jnp.int32).astype(jnp.int16)


def decode_square(code):
    code = code.astype(jnp.int32).astype(jnp.float32)
    value = code[:SCALE_ROW] * (scale_of(code[SCALE_ROW : SCALE_ROW + 1]) * np.float32(1.0 / 32700.0))
    return value * value


def full_rows(value):
    return jnp.concatenate([value, jnp.zeros((PIECE_ROWS - SCALE_ROW, 128), jnp.float32)], 0)


def density_kernel(
    counts_ref, coarse_hbm, waves_hbm, flags_ref, key1_ref, key2_ref, sum_code,
    coarse_ref, waves_ref, coarse_pack_ref, coarse_halo_ref, pack_ref, halo_ref, level_ref, fine_ref, spill_ref, spilled_ref,
    x_ref, a_ref, b_ref, part_a_ref, part_b_ref, coef_ref, value_ref, code_ref, got_outer, got_middle,
    load_sem, halo_send, halo_recv, code_send, outer_recv, middle_recv, sum_send, sum_recv, *, count, ranges, table, valued
):
    boxes = coarse_hbm.shape[-1]
    pieces = code_ref.shape[0]
    tiles = pieces // PARTS
    me, position = lax.axis_index("orb"), lax.axis_index("box")
    after, before = lax.rem(position + 1, ranges), lax.rem(position + ranges - 1, ranges)
    half = count // 2
    inward = jnp.where(me < half, me + 1, me - 1)
    outward = jnp.where(me < half, me - 1, me + 1)
    outermost = (me == 0) | (me == count - 1)
    middle = (me == half - 1) | (me == half)
    first_range, last_range = position == 0, position == ranges - 1
    mesh_id = pl.DeviceIdType.MESH
    load_coarse = pltpu.make_async_copy(coarse_hbm, coarse_ref.at[pl.ds(0, ROWS)], load_sem.at[0])
    load_waves = pltpu.make_async_copy(waves_hbm, waves_ref, load_sem.at[1])
    load_coarse.start()
    load_waves.start()
    barrier = pltpu.get_barrier_semaphore()
    for d in range(1, count):
        pl.semaphore_signal(barrier, inc=1, device_id={"orb": lax.rem(me + d, count)}, device_id_type=mesh_id)
    for other in (after, before):
        pl.semaphore_signal(barrier, inc=1, device_id={"box": other}, device_id_type=mesh_id)

    def remote(source, target, sends, recvs, device):
        return pltpu.make_async_remote_copy(
            src_ref=source,
            dst_ref=target,
            send_sem=sends,
            recv_sem=recvs,
            device_id=device,
            device_id_type=mesh_id,
        )

    def halo(source, target, index):
        return remote(source, target, halo_send.at[index], halo_recv.at[index], {"box": after})

    def to_outer_slot(n):
        return remote(code_ref.at[n], got_outer.at[n], code_send.at[n], outer_recv.at[n], {"orb": inward})

    def to_middle_slot(n):
        return remote(code_ref.at[n], got_middle.at[n], code_send.at[n], middle_recv.at[n], {"orb": inward})

    def to_total(n):
        return remote(sum_code.at[n], sum_code.at[n], sum_send.at[n], sum_recv.at[n], {"orb": outward})

    def when_not(condition):
        return pl.when(jnp.logical_not(condition))

    def send_halo(copy):
        @when_not(last_range)
        def send():
            copy.start()

    def wait_halo(copy):
        @when_not(first_range)
        def wait():
            copy.wait_recv()

    def send_partial(n, value):
        code_ref[n] = encode(value)

        @pl.when(middle)
        def exchange():
            to_middle_slot(n).start()

        @when_not(middle)
        def pass_in():
            to_outer_slot(n).start()

    def combine(n):
        @when_not(outermost)
        def add():
            to_outer_slot(n).wait_recv()
            own = value_ref[n]
            total = full_rows(decode_square(got_outer[n])) + own * own
            send_partial(n, jnp.sqrt(total))

    def finish(n):
        @pl.when(middle)
        def close():
            to_middle_slot(n).wait_recv()
            total = decode_square(code_ref[n]) + decode_square(got_middle[n])
            sum_code[n] = encode(full_rows(jnp.sqrt(2.0 * total)))

        @when_not(middle | outermost)
        def receive():
            to_total(n).wait_recv()

        @when_not(outermost)
        def pass_out():
            to_total(n).start()

    coarse_halo = [halo(coarse_pack_ref.at[h], coarse_halo_ref.at[h], h) for h in range(2)]
    waves_halo = halo(pack_ref, halo_ref, 2)
    fine_halo = halo(spill_ref, spilled_ref, 3)

    @pl.when(first_range)
    def no_halo():
        for ref in (coarse_halo_ref, halo_ref, spilled_ref):
            ref[...] = jnp.zeros(ref.shape, ref.dtype)

    keep = jnp.broadcast_to((1 - flags_ref[...]).astype(jnp.float32), (16, boxes)).astype(jnp.bfloat16)
    spread = [spread_matrix(boxes, g) for g in range(4)]
    tail = 8 * SEGMENT - ROWS
    coarse_ref[ROWS : ROWS + tail] = jnp.zeros((tail, 8, boxes), jnp.bfloat16)

    def segment(index):
        return coarse_ref[SEGMENT * index : SEGMENT * (index + 1)].reshape(8 * SEGMENT, boxes)

    load_coarse.wait()
    for h in range(2):
        total = dot(segment(4 * h), spread[0])
        for g in range(1, 4):
            total = total + dot(segment(4 * h + g), spread[g])
        coarse_pack_ref[h] = total.astype(jnp.bfloat16)
        if h == 0:
            pl.semaphore_wait(barrier, count + 1)
        send_halo(coarse_halo[h])
    load_waves.wait()
    packed_keep = sum(dot(keep, s) for s in spread)[:1]
    for h in range(2):
        total = None
        for g in range(4):
            if 4 * h + g > 0:
                term = dot(waves_ref[0, 4 * h + g - 1], spread[g])
                total = term if total is None else total + term
        pack_ref[h] = (total * packed_keep).astype(jnp.bfloat16)
    send_halo(waves_halo)
    column, octant = local_keys(key1_ref[...], boxes)
    fill_coefficients(coef_ref.at[tiles], octant, table)
    own = pick_own(column, boxes)
    fine_ref[ROWS - 1 : 4 * QUARTER, :] = jnp.zeros((4 * QUARTER - ROWS + 1, 128), jnp.float32)
    pad = PIECE_ROWS - PIECE + 3
    value_ref[:, PIECE_ROWS - pad : PIECE_ROWS, :] = jnp.zeros((pieces, pad, 128), jnp.float32)

    def leaf_coefficients(t, carry):
        fill_coefficients(coef_ref.at[t], local_keys(key2_ref[t], boxes)[1], valued)
        return carry

    lax.fori_loop(0, tiles, leaf_coefficients, 0)
    coef = coef_ref.at[tiles]
    for h in range(2):
        wait_halo(coarse_halo[h])
        for g in range(4):
            pick = jnp.concatenate([own, pick_spilled(column, g)], 0).astype(jnp.bfloat16)
            both = jnp.concatenate([segment(4 * h + g), coarse_halo_ref[h]], 1)
            start = 8 * SEGMENT * (4 * h + g)
            level_ref[start : start + 8 * SEGMENT, :] = dot(both, pick)
        lower_axis(level_ref, a_ref, coef, 0, 0, 4, HALVES[h])
    lower_axis(a_ref, b_ref, coef, 1, 0, 2)

    def store_fine(row, rows_in, value):
        fine_ref[row : row + rows_in, :] = value[:rows_in]

    contract(b_ref, 0, 1, coef, 2, store_fine)
    for part in range(2):
        total = None
        for g in range(4):
            quarter = fine_ref[QUARTER * g : QUARTER * (g + 1), :]
            half_value = quarter.astype(jnp.bfloat16)
            if part == 1:
                half_value = (quarter - half_value.astype(jnp.float32)).astype(jnp.bfloat16)
            term = dot(half_value, spread[g])
            total = term if total is None else total + term
        spill_ref[part] = total.astype(jnp.bfloat16)
    send_halo(fine_halo)

    columns = jnp.concatenate([local_keys(key2_ref[t], boxes)[0] for t in range(tiles)], 1)
    own = pick_own(columns, boxes)
    own_kept = own * dot(keep, own.astype(jnp.bfloat16))[:1]

    def store_blocks(block, start, rows_in, value):
        for t in range(tiles):
            x_ref[t, block, start : start + rows_in, :] = value[:, 128 * t : 128 * (t + 1)]

    wait_halo(waves_halo)
    for g in range(4):
        pick = jnp.concatenate([own_kept, pick_spilled(columns, g)], 0).astype(jnp.bfloat16)
        for h in range(2):
            if 4 * h + g > 0:
                both = jnp.concatenate([waves_ref[0, 4 * h + g - 1], halo_ref[h]], 1)
                store_blocks(4 * h + g, 0, ROWS, dot(both, pick))

    def leaf_axis(t, part, start, stop):
        lower_axis(
            x_ref.at[t], part_a_ref.at[part], coef_ref.at[t], 0, start, stop, first=3 * part, outputs=3
        )

    for part in range(PARTS):
        leaf_axis(0, part, 1, 4)
    wait_halo(fine_halo)
    for g in range(4):
        pick = jnp.concatenate([own, pick_spilled(columns, g)], 0).astype(jnp.bfloat16)
        quarter = fine_ref[QUARTER * g : QUARTER * (g + 1), :]
        high = quarter.astype(jnp.bfloat16)
        low = (quarter - high.astype(jnp.float32)).astype(jnp.bfloat16)
        total = dot(jnp.concatenate([high, spilled_ref[0]], 1), pick)
        total = total + dot(jnp.concatenate([low, spilled_ref[1]], 1), pick)
        store_blocks(0, QUARTER * g, QUARTER, total)
    for n in range(pieces):
        t, part = n // PARTS, n % PARTS
        leaf_axis(t, part, 0, 1 if t == 0 else 4)
        kinds = dict(groups=THIRD_GROUPS, width=WIDTH)
        lower_axis(part_a_ref.at[part], part_b_ref, coef_ref.at[t], 1, 0, 2, **kinds)
        slot = t * 128 + lax.broadcasted_iota(jnp.int32, (8, 128), 1)
        live = jnp.where(slot < counts_ref[0], 1.0, 0.0).astype(jnp.float32)

        def store_value(row, rows_in, value):
            value_ref[n, row : row + rows_in, :] = (value * live)[:rows_in]

        contract(part_b_ref, 0, 1, coef_ref.at[t], 2, store_value, **kinds)

        @pl.when(outermost)
        def start_chain():
            send_partial(n, value_ref[n])

        if n >= LAG:
            combine(n - LAG)
        if n >= 2 * LAG:
            finish(n - 2 * LAG)
    for n in range(pieces, pieces + 2 * LAG):
        if 0 <= n - LAG < pieces:
            combine(n - LAG)
        if 0 <= n - 2 * LAG:
            finish(n - 2 * LAG)

    @when_not(last_range)
    def halos_sent():
        for copy in (*coarse_halo, waves_halo, fine_halo):
            copy.wait_send()

    for n in range(pieces):
        to_outer_slot(n).wait_send()

        @when_not(outermost)
        def totals_sent():
            to_total(n).wait_send()

        @pl.when(outermost & jnp.logical_not(middle))
        def totals_received():
            to_total(n).wait_recv()


def decode_kernel(code_ref, out_hbm, piece_ref, value_ref, sem):
    pieces = code_ref.shape[0]
    tiles = pieces // PARTS

    def out_copy(t):
        return pltpu.make_async_copy(
            value_ref.at[t, pl.ds(0, ROWS)], out_hbm.at[:, pl.ds(128 * t, 128)], sem.at[t]
        )

    for n in range(pieces):
        piece_ref[n, 0:SCALE_ROW, :] = decode_square(code_ref[n])
    for n in range(pieces):
        t, part = n // PARTS, n % PARTS
        for f in range(3):
            for k in range(11):
                rows = min(8, 81 - 8 * k)
                value = piece_ref[n, pl.ds(24 * k + f, rows, stride=3), :]
                value_ref[t, pl.ds(72 * k + 3 * part + f, rows, stride=9), :] = value
        if part == PARTS - 1:
            out_copy(t).start()
    for t in range(tiles):
        out_copy(t).wait()


def shards(coarse, wavelets, leaf_flags, child_key1, child_key2, counts):
    matrix, quad = wavelet_tables()
    valued = np.einsum("kop,gp->kog", matrix, quad)
    boxes = coarse.shape[-1]
    slots = child_key2.shape[0]
    count, ranges = lax.axis_size("orb"), lax.axis_size("box")
    tiles = slots // 128
    pieces = PARTS * tiles
    vmem = pl.BlockSpec(memory_space=pltpu.VMEM)
    anywhere = pl.BlockSpec(memory_space=pltpu.HBM)
    codes = pl.pallas_call(
        lambda *refs: density_kernel(*refs, count=count, ranges=ranges, table=matrix, valued=valued),
        out_shape=jax.ShapeDtypeStruct((pieces, PIECE_ROWS, 128), jnp.int16),
        in_specs=[pl.BlockSpec(memory_space=pltpu.SMEM), anywhere, anywhere, vmem, vmem, vmem],
        out_specs=vmem,
        scratch_shapes=[
            pltpu.VMEM((8 * SEGMENT, 8, boxes), jnp.bfloat16),
            pltpu.VMEM(wavelets.shape, jnp.bfloat16),
            pltpu.VMEM((2, 8 * SEGMENT, 128), jnp.bfloat16),
            pltpu.VMEM((2, 8 * SEGMENT, 128), jnp.bfloat16),
            pltpu.VMEM((2, ROWS, 128), jnp.bfloat16),
            pltpu.VMEM((2, ROWS, 128), jnp.bfloat16),
            pltpu.VMEM((8 * PADDED, 128), jnp.float32),
            pltpu.VMEM((4 * QUARTER, 128), jnp.float32),
            pltpu.VMEM((2, QUARTER, 128), jnp.bfloat16),
            pltpu.VMEM((2, QUARTER, 128), jnp.bfloat16),
            pltpu.VMEM((tiles, 8, PADDED, 128), jnp.float32),
            pltpu.VMEM((4, PADDED, 128), jnp.float32),
            pltpu.VMEM((2, PADDED, 128), jnp.float32),
            pltpu.VMEM((PARTS, 4, PART_ROWS, 128), jnp.float32),
            pltpu.VMEM((2, PART_ROWS, 128), jnp.float32),
            pltpu.VMEM((tiles + 1, 3 * 162, 8, 128), jnp.float32),
            pltpu.VMEM((pieces, PIECE_ROWS, 128), jnp.float32),
            pltpu.VMEM((pieces, PIECE_ROWS, 128), jnp.int16),
            pltpu.VMEM((pieces, PIECE_ROWS, 128), jnp.int16),
            pltpu.VMEM((pieces, PIECE_ROWS, 128), jnp.int16),
            pltpu.SemaphoreType.DMA((2,)),
            pltpu.SemaphoreType.DMA((4,)),
            pltpu.SemaphoreType.DMA((4,)),
        ]
        + [pltpu.SemaphoreType.DMA((pieces,))] * 5,
        compiler_params=pltpu.CompilerParams(
            collective_id=0, has_side_effects=True, vmem_limit_bytes=60 * 1024 * 1024
        ),
    )(
        counts,
        jnp.transpose(coarse[0], (1, 0, 2)),
        wavelets,
        leaf_flags,
        child_key1.reshape(1, boxes),
        child_key2.reshape(tiles, 1, 128),
    )
    return pl.pallas_call(
        decode_kernel,
        out_shape=jax.ShapeDtypeStruct((ROWS, slots), jnp.float32),
        in_specs=[vmem],
        out_specs=anywhere,
        scratch_shapes=[
            pltpu.VMEM((pieces, PIECE_ROWS, 128), jnp.float32),
            pltpu.VMEM((tiles, PADDED, 128), jnp.float32),
            pltpu.SemaphoreType.DMA((tiles,)),
        ],
    )(codes)


def solution(mesh):
    in_specs = (
        P("orb", None, None, "box"),
        P("orb", None, None, "box"),
        P("orb", "box"),
        P("box"),
        P("box"),
        P("box"),
    )
    out_specs = P(None, "box")
    return jax.shard_map(shards, mesh=mesh, in_specs=in_specs, out_specs=out_specs, check_vma=False)
```

```python
import math

import jax
import jax.numpy as jnp
import numpy as np
from jax import lax
from jax.experimental import pallas as pl
from jax.experimental.pallas import tpu as pltpu
from jax.sharding import PartitionSpec as P

SPILL = 32


def legendre_pair(order, where):
    before = where * 0.0 + 1.0
    value = where
    for degree in range(1, order):
        before, value = (value, ((2 * degree + 1) * where * value - degree * before) / (degree + 1))
    return (value, before)


def gauss_rule(order):
    nodes = np.cos(np.pi * (np.arange(order) + 0.75) / (order + 0.5))
    for repeat in range(40):
        value, before = legendre_pair(order, nodes)
        slope = order * (nodes * value - before) / (nodes * nodes - 1.0)
        nodes = nodes - value / slope
    value, before = legendre_pair(order, nodes)
    slope = order * (nodes * value - before) / (nodes * nodes - 1.0)
    weights = 2.0 / ((1.0 - nodes * nodes) * slope * slope)
    return (nodes[::-1], weights[::-1])


def legendre_basis(where):
    shifted = 2.0 * where - 1.0
    rows = [shifted * 0.0 + 1.0, shifted]
    for degree in range(1, 8):
        rows.append(
            ((2 * degree + 1) * shifted * rows[degree] - degree * rows[degree - 1]) / (degree + 1)
        )
    scale = np.sqrt(2.0 * np.arange(9) + 1.0)[:, None]
    return np.stack(rows, 0) * scale


def complement_rows(scaling_rows):
    members = [scaling_rows[index] for index in range(9)]
    kept = []
    identity = np.eye(18)
    for column in range(18):
        vector = identity[column]
        for passes in range(2):
            for member in members + kept:
                vector = vector - np.dot(member, vector) * member
        length = np.sqrt(np.dot(vector, vector))
        if length > 0.1 and len(kept) < 9:
            kept.append(vector / length)
    return np.stack(kept, 0)


def wavelet_tables():
    nodes, weights = gauss_rule(24)
    points = 0.5 * (nodes + 1.0)
    halves = 0.5 * weights
    lower = legendre_basis(0.5 * points) * halves @ legendre_basis(points).T / math.sqrt(2.0)
    upper = legendre_basis(0.5 * points + 0.5) * halves @ legendre_basis(points).T / math.sqrt(2.0)
    scaling_rows = np.concatenate([lower, upper], 1)
    wavelet_rows = complement_rows(scaling_rows)
    matrix = np.concatenate([scaling_rows, wavelet_rows], 0).reshape(2, 9, 2, 9)
    gauss, gauss_weights = gauss_rule(9)
    quad = legendre_basis(0.5 * (gauss + 1.0)).T * np.sqrt(0.5 * gauss_weights)[:, None]
    return (matrix.reshape(18, 2, 9), quad)


ROWS = 729
PADDED = 800
SEGMENT = 92
HALVES = (((0, 1), (2, 3, 4)), ((5, 6), (7, 8), (9, 10)))
GROUPS = ((0, 1), (2, 3), (4, 5), (6, 7), (8, 9, 10))
THIRD_GROUPS = ((0, 1), (2, 3))
QUARTER = 192
PARTS = 3
WIDTH = 27
PIECE = 243
PIECE_ROWS = 256
SPLITS = ((0, 112), (112, 256))
SHIFT = 4
PART_ROWS = 288
LAG = 2


def local_keys(keys, boxes):
    key = keys - lax.axis_index("box") * (8 * boxes)
    return (lax.shift_right_arithmetic(key, 3), key & 7)


def spread_matrix(boxes, group):
    source = lax.broadcasted_iota(jnp.int32, (boxes, 128), 0)
    target = lax.broadcasted_iota(jnp.int32, (boxes, 128), 1)
    hit = (source - (boxes - SPILL) == target - SPILL * group) & (source >= boxes - SPILL)
    return hit.astype(jnp.float32).astype(jnp.bfloat16)


def pick_own(column, boxes):
    row = lax.broadcasted_iota(jnp.int32, (boxes, column.shape[1]), 0)
    return (row == column).astype(jnp.float32)


def pick_spilled(column, group):
    row = lax.broadcasted_iota(jnp.int32, (128, column.shape[1]), 0)
    hit = (row == column + SPILL * (group + 1)) & (column < 0)
    return hit.astype(jnp.float32)


def fill_coefficients(coef_ref, octant, table):
    for axis in range(3):
        bit = jnp.broadcast_to((octant >> axis) & 1, (8, 128)) == 1
        for k in range(18):
            for f in range(9):
                coef_ref[axis * 162 + k * 9 + f] = jnp.where(
                    bit, np.float32(table[k, 1, f]), np.float32(table[k, 0, f])
                )


def contract(source_ref, low, high, coef_ref, axis, store, groups=GROUPS, first=0, outputs=9, width=81):
    def load(block, row):
        if len(source_ref.shape) == 2:
            return source_ref[pl.ds(8 * row + block, 8, stride=72), :]
        return source_ref[block, pl.ds(row, 8, stride=9), :]

    for group in groups:
        inputs = [[load(block, l + 72 * t) for block in (low, high) for l in range(9)] for t in group]
        for f in range(outputs):
            sums = [None] * len(group)
            for k in range(18):
                weight = coef_ref[axis * 162 + k * 9 + first + f]
                for n in range(len(group)):
                    term = weight * inputs[n][k]
                    sums[n] = term if sums[n] is None else sums[n] + term
            for n, t in enumerate(group):
                store(width * f + 8 * t, min(8, width - 8 * t), sums[n])


def lower_axis(source_ref, target_ref, coef_ref, axis, start, stop, groups=GROUPS, **kinds):
    def step(index, carry):
        def store(row, count, value):
            target_ref[index, row : row + count, :] = value[:count]

        contract(source_ref, 2 * index, 2 * index + 1, coef_ref, axis, store, groups, **kinds)
        return carry

    lax.fori_loop(start, stop, step, 0)


def dot(left, right):
    return jnp.dot(left, right, preferred_element_type=jnp.float32)


def scale_of(steps):
    return jnp.exp2(steps * np.float32(1.0 / 256.0))


def encode(value):
    rows = value.shape[0]
    last = lax.broadcasted_iota(jnp.int32, (8, 128), 0) == 7
    top = jnp.maximum(jnp.max(jnp.abs(value), axis=0, keepdims=True), 1e-30)
    steps = jnp.ceil(jnp.log2(top) * 256.0)
    code = jnp.round(value * (32700.0 / scale_of(steps)))
    code = jnp.concatenate([code[: rows - 8], jnp.where(last, steps, code[rows - 8 :])], 0)
    return code.astype(jnp.int32).astype(jnp.int16)


def decode_square(code):
    rows = code.shape[0]
    last = lax.broadcasted_iota(jnp.int32, (8, 128), 0) == 7
    code = code.astype(jnp.int32).astype(jnp.float32)
    value = code * (scale_of(code[rows - 1 : rows]) * np.float32(1.0 / 32700.0))
    value = jnp.concatenate([value[: rows - 8], jnp.where(last, 0.0, value[rows - 8 :])], 0)
    return value * value


def spread_row(row):
    return row + (SHIFT if row >= 4 * WIDTH else 0)


def density_kernel(
    counts_ref, coarse_hbm, waves_hbm, flags_ref, key1_ref, key2_ref, sum_code,
    coarse_ref, waves_ref, coarse_pack_ref, coarse_halo_ref, pack_ref, halo_ref, level_ref, fine_ref, spill_ref, spilled_ref,
    x_ref, a_ref, b_ref, part_a_ref, part_b_ref, coef_ref, value_ref, code_ref, got_outer, got_middle,
    load_sem, halo_send, halo_recv, code_send, outer_recv, middle_recv, sum_send, sum_recv, *, count, ranges, table, valued
):
    boxes = coarse_hbm.shape[-1]
    pieces = code_ref.shape[0]
    tiles = pieces // PARTS
    me, position = lax.axis_index("orb"), lax.axis_index("box")
    after, before = lax.rem(position + 1, ranges), lax.rem(position + ranges - 1, ranges)
    half = count // 2
    inward = jnp.where(me < half, me + 1, me - 1)
    outward = jnp.where(me < half, me - 1, me + 1)
    outermost = (me == 0) | (me == count - 1)
    middle = (me == half - 1) | (me == half)
    first_range, last_range = position == 0, position == ranges - 1
    mesh_id = pl.DeviceIdType.MESH
    load_coarse = pltpu.make_async_copy(coarse_hbm, coarse_ref.at[pl.ds(0, ROWS)], load_sem.at[0])
    load_waves = pltpu.make_async_copy(waves_hbm, waves_ref, load_sem.at[1])
    load_coarse.start()
    load_waves.start()
    barrier = pltpu.get_barrier_semaphore()
    pl.semaphore_signal(barrier, inc=1, device_id={"orb": inward}, device_id_type=mesh_id)

    @pl.when(jnp.logical_not(outermost))
    def greet_outward():
        pl.semaphore_signal(barrier, inc=1, device_id={"orb": outward}, device_id_type=mesh_id)

    @pl.when(jnp.logical_not(first_range))
    def greet_before():
        pl.semaphore_signal(barrier, inc=1, device_id={"box": before}, device_id_type=mesh_id)

    def remote(source, target, sends, recvs, device):
        return pltpu.make_async_remote_copy(
            src_ref=source,
            dst_ref=target,
            send_sem=sends,
            recv_sem=recvs,
            device_id=device,
            device_id_type=mesh_id,
        )

    def halo(source, target, index):
        return remote(source, target, halo_send.at[index], halo_recv.at[index], {"box": after})

    def part_of(ref, n, s):
        return ref.at[n, pl.ds(SPLITS[s][0], SPLITS[s][1] - SPLITS[s][0])]

    def inner_copy(slots, recvs, n, s):
        return remote(part_of(code_ref, n, s), part_of(slots, n, s), code_send.at[n, s], recvs.at[n, s], {"orb": inward})

    def to_outer_slot(n, s):
        return inner_copy(got_outer, outer_recv, n, s)

    def to_middle_slot(n, s):
        return inner_copy(got_middle, middle_recv, n, s)

    def to_total(n, s):
        part = part_of(sum_code, n, s)
        return remote(part, part, sum_send.at[n, s], sum_recv.at[n, s], {"orb": outward})

    def when_not(condition):
        return pl.when(jnp.logical_not(condition))

    def send_halo(copy):
        @when_not(last_range)
        def send():
            copy.start()

    def wait_halo(copy):
        @when_not(first_range)
        def wait():
            copy.wait_recv()

    def send_partial(n, s, value):
        start, stop = SPLITS[s]
        code_ref[n, start:stop] = encode(value)

        @pl.when(middle)
        def exchange():
            to_middle_slot(n, s).start()

        @when_not(middle)
        def pass_in():
            to_outer_slot(n, s).start()

    def combine(n):
        @when_not(outermost)
        def add():
            for s, (start, stop) in enumerate(SPLITS):
                to_outer_slot(n, s).wait_recv()
                own = value_ref[n, start:stop]
                send_partial(n, s, jnp.sqrt(decode_square(got_outer[n, start:stop]) + own * own))

    def finish(n):
        for s, (start, stop) in enumerate(SPLITS):

            @pl.when(middle)
            def close():
                to_middle_slot(n, s).wait_recv()
                total = decode_square(code_ref[n, start:stop]) + decode_square(got_middle[n, start:stop])
                sum_code[n, start:stop] = encode(jnp.sqrt(2.0 * total))

            @when_not(middle | outermost)
            def receive():
                to_total(n, s).wait_recv()

            @when_not(outermost)
            def pass_out():
                to_total(n, s).start()

    coarse_halo = [halo(coarse_pack_ref.at[h], coarse_halo_ref.at[h], h) for h in range(2)]
    waves_halo = halo(pack_ref, halo_ref, 2)
    fine_halo = halo(spill_ref, spilled_ref, 3)

    @pl.when(first_range)
    def no_halo():
        for ref in (coarse_halo_ref, halo_ref, spilled_ref):
            ref[...] = jnp.zeros(ref.shape, ref.dtype)

    keep = jnp.broadcast_to((1 - flags_ref[...]).astype(jnp.float32), (16, boxes)).astype(jnp.bfloat16)
    spread = [spread_matrix(boxes, g) for g in range(4)]
    tail = 8 * SEGMENT - ROWS
    coarse_ref[ROWS : ROWS + tail] = jnp.zeros((tail, 8, boxes), jnp.bfloat16)

    def segment(index):
        return coarse_ref[SEGMENT * index : SEGMENT * (index + 1)].reshape(8 * SEGMENT, boxes)

    load_coarse.wait()
    for h in range(2):
        total = dot(segment(4 * h), spread[0])
        for g in range(1, 4):
            total = total + dot(segment(4 * h + g), spread[g])
        coarse_pack_ref[h] = total.astype(jnp.bfloat16)
        if h == 0:
            pl.semaphore_wait(barrier, 1 + jnp.where(outermost, 0, 1) + jnp.where(last_range, 0, 1))
        send_halo(coarse_halo[h])
    load_waves.wait()
    packed_keep = sum(dot(keep, s) for s in spread)[:1]
    for h in range(2):
        total = None
        for g in range(4):
            if 4 * h + g > 0:
                term = dot(waves_ref[0, 4 * h + g - 1], spread[g])
                total = term if total is None else total + term
        pack_ref[h] = (total * packed_keep).astype(jnp.bfloat16)
    send_halo(waves_halo)
    column, octant = local_keys(key1_ref[...], boxes)
    fill_coefficients(coef_ref.at[tiles], octant, table)
    own = pick_own(column, boxes)
    fine_ref[ROWS - 1 : 4 * QUARTER, :] = jnp.zeros((4 * QUARTER - ROWS + 1, 128), jnp.float32)
    for start in (4 * WIDTH - 4, PIECE_ROWS - 16):
        stop = min(start + 16, PIECE_ROWS)
        value_ref[:, start:stop, :] = jnp.zeros((pieces, stop - start, 128), jnp.float32)

    def leaf_coefficients(t, carry):
        fill_coefficients(coef_ref.at[t], local_keys(key2_ref[t], boxes)[1], valued)
        return carry

    lax.fori_loop(0, tiles, leaf_coefficients, 0)
    coef = coef_ref.at[tiles]
    for h in range(2):
        wait_halo(coarse_halo[h])
        for g in range(4):
            pick = jnp.concatenate([own, pick_spilled(column, g)], 0).astype(jnp.bfloat16)
            both = jnp.concatenate([segment(4 * h + g), coarse_halo_ref[h]], 1)
            start = 8 * SEGMENT * (4 * h + g)
            level_ref[start : start + 8 * SEGMENT, :] = dot(both, pick)
        lower_axis(level_ref, a_ref, coef, 0, 0, 4, HALVES[h])
    lower_axis(a_ref, b_ref, coef, 1, 0, 2)

    def store_fine(row, rows_in, value):
        fine_ref[row : row + rows_in, :] = value[:rows_in]

    contract(b_ref, 0, 1, coef, 2, store_fine)
    for part in range(2):
        total = None
        for g in range(4):
            quarter = fine_ref[QUARTER * g : QUARTER * (g + 1), :]
            half_value = quarter.astype(jnp.bfloat16)
            if part == 1:
                half_value = (quarter - half_value.astype(jnp.float32)).astype(jnp.bfloat16)
            term = dot(half_value, spread[g])
            total = term if total is None else total + term
        spill_ref[part] = total.astype(jnp.bfloat16)
    send_halo(fine_halo)

    columns = jnp.concatenate([local_keys(key2_ref[t], boxes)[0] for t in range(tiles)], 1)
    own = pick_own(columns, boxes)
    own_kept = own * dot(keep, own.astype(jnp.bfloat16))[:1]

    def store_blocks(block, start, rows_in, value):
        for t in range(tiles):
            x_ref[t, block, start : start + rows_in, :] = value[:, 128 * t : 128 * (t + 1)]

    wait_halo(waves_halo)
    for g in range(4):
        pick = jnp.concatenate([own_kept, pick_spilled(columns, g)], 0).astype(jnp.bfloat16)
        for h in range(2):
            if 4 * h + g > 0:
                both = jnp.concatenate([waves_ref[0, 4 * h + g - 1], halo_ref[h]], 1)
                store_blocks(4 * h + g, 0, ROWS, dot(both, pick))

    def leaf_axis(t, part, start, stop):
        lower_axis(
            x_ref.at[t], part_a_ref.at[part], coef_ref.at[t], 0, start, stop, first=3 * part, outputs=3
        )

    for part in range(PARTS):
        leaf_axis(0, part, 1, 4)
    wait_halo(fine_halo)
    for g in range(4):
        pick = jnp.concatenate([own, pick_spilled(columns, g)], 0).astype(jnp.bfloat16)
        quarter = fine_ref[QUARTER * g : QUARTER * (g + 1), :]
        high = quarter.astype(jnp.bfloat16)
        low = (quarter - high.astype(jnp.float32)).astype(jnp.bfloat16)
        total = dot(jnp.concatenate([high, spilled_ref[0]], 1), pick)
        total = total + dot(jnp.concatenate([low, spilled_ref[1]], 1), pick)
        store_blocks(0, QUARTER * g, QUARTER, total)
    for n in range(pieces):
        t, part = n // PARTS, n % PARTS
        leaf_axis(t, part, 0, 1 if t == 0 else 4)
        kinds = dict(groups=THIRD_GROUPS, width=WIDTH)
        lower_axis(part_a_ref.at[part], part_b_ref, coef_ref.at[t], 1, 0, 2, **kinds)
        slot = t * 128 + lax.broadcasted_iota(jnp.int32, (8, 128), 1)
        live = jnp.where(slot < counts_ref[0], 1.0, 0.0).astype(jnp.float32)

        def store_value(row, rows_in, value):
            row = spread_row(row)
            value_ref[n, row : row + rows_in, :] = (value * live)[:rows_in]

        contract(part_b_ref, 0, 1, coef_ref.at[t], 2, store_value, **kinds)

        @pl.when(outermost)
        def start_chain():
            for s, (start, stop) in enumerate(SPLITS):
                send_partial(n, s, value_ref[n, start:stop])

        if n >= LAG:
            combine(n - LAG)
        if n >= 2 * LAG:
            finish(n - 2 * LAG)
    for n in range(pieces, pieces + 2 * LAG):
        if 0 <= n - LAG < pieces:
            combine(n - LAG)
        if 0 <= n - 2 * LAG:
            finish(n - 2 * LAG)

    @when_not(last_range)
    def halos_sent():
        for copy in (*coarse_halo, waves_halo, fine_halo):
            copy.wait_send()

    for n in range(pieces):
        for s in range(len(SPLITS)):
            to_outer_slot(n, s).wait_send()

            @when_not(outermost)
            def totals_sent():
                to_total(n, s).wait_send()

            @pl.when(outermost & jnp.logical_not(middle))
            def totals_received():
                to_total(n, s).wait_recv()


def decode_kernel(code_ref, out_hbm, piece_ref, value_ref, sem):
    pieces = code_ref.shape[0]
    tiles = pieces // PARTS

    def out_copy(t):
        return pltpu.make_async_copy(
            value_ref.at[t, pl.ds(0, ROWS)], out_hbm.at[:, pl.ds(128 * t, 128)], sem.at[t]
        )

    for n in range(pieces):
        for start, stop in SPLITS:
            piece_ref[n, start:stop, :] = decode_square(code_ref[n, start:stop])
    for n in range(pieces):
        t, part = n // PARTS, n % PARTS
        for f in range(3):
            for k in (*range(0, 36, 8), *range(36, 81, 8)):
                rows = min(8, (36 if k < 36 else 81) - k)
                value = piece_ref[n, pl.ds(spread_row(3 * k + f), rows, stride=3), :]
                value_ref[t, pl.ds(9 * k + 3 * part + f, rows, stride=9), :] = value
        if part == PARTS - 1:
            out_copy(t).start()
    for t in range(tiles):
        out_copy(t).wait()


def shards(coarse, wavelets, leaf_flags, child_key1, child_key2, counts):
    matrix, quad = wavelet_tables()
    valued = np.einsum("kop,gp->kog", matrix, quad)
    boxes = coarse.shape[-1]
    slots = child_key2.shape[0]
    count, ranges = lax.axis_size("orb"), lax.axis_size("box")
    tiles = slots // 128
    pieces = PARTS * tiles
    vmem = pl.BlockSpec(memory_space=pltpu.VMEM)
    anywhere = pl.BlockSpec(memory_space=pltpu.HBM)
    codes = pl.pallas_call(
        lambda *refs: density_kernel(*refs, count=count, ranges=ranges, table=matrix, valued=valued),
        out_shape=jax.ShapeDtypeStruct((pieces, PIECE_ROWS, 128), jnp.int16),
        in_specs=[pl.BlockSpec(memory_space=pltpu.SMEM), anywhere, anywhere, vmem, vmem, vmem],
        out_specs=vmem,
        scratch_shapes=[
            pltpu.VMEM((8 * SEGMENT, 8, boxes), jnp.bfloat16),
            pltpu.VMEM(wavelets.shape, jnp.bfloat16),
            pltpu.VMEM((2, 8 * SEGMENT, 128), jnp.bfloat16),
            pltpu.VMEM((2, 8 * SEGMENT, 128), jnp.bfloat16),
            pltpu.VMEM((2, ROWS, 128), jnp.bfloat16),
            pltpu.VMEM((2, ROWS, 128), jnp.bfloat16),
            pltpu.VMEM((8 * PADDED, 128), jnp.float32),
            pltpu.VMEM((4 * QUARTER, 128), jnp.float32),
            pltpu.VMEM((2, QUARTER, 128), jnp.bfloat16),
            pltpu.VMEM((2, QUARTER, 128), jnp.bfloat16),
            pltpu.VMEM((tiles, 8, PADDED, 128), jnp.float32),
            pltpu.VMEM((4, PADDED, 128), jnp.float32),
            pltpu.VMEM((2, PADDED, 128), jnp.float32),
            pltpu.VMEM((PARTS, 4, PART_ROWS, 128), jnp.float32),
            pltpu.VMEM((2, PART_ROWS, 128), jnp.float32),
            pltpu.VMEM((tiles + 1, 3 * 162, 8, 128), jnp.float32),
            pltpu.VMEM((pieces, PIECE_ROWS, 128), jnp.float32),
            pltpu.VMEM((pieces, PIECE_ROWS, 128), jnp.int16),
            pltpu.VMEM((pieces, PIECE_ROWS, 128), jnp.int16),
            pltpu.VMEM((pieces, PIECE_ROWS, 128), jnp.int16),
            pltpu.SemaphoreType.DMA((2,)),
            pltpu.SemaphoreType.DMA((4,)),
            pltpu.SemaphoreType.DMA((4,)),
        ]
        + [pltpu.SemaphoreType.DMA((pieces, len(SPLITS)))] * 5,
        compiler_params=pltpu.CompilerParams(
            collective_id=0, has_side_effects=True, vmem_limit_bytes=60 * 1024 * 1024
        ),
    )(
        counts,
        jnp.transpose(coarse[0], (1, 0, 2)),
        wavelets,
        leaf_flags,
        child_key1.reshape(1, boxes),
        child_key2.reshape(tiles, 1, 128),
    )
    return pl.pallas_call(
        decode_kernel,
        out_shape=jax.ShapeDtypeStruct((ROWS, slots), jnp.float32),
        in_specs=[vmem],
        out_specs=anywhere,
        scratch_shapes=[
            pltpu.VMEM((pieces, PIECE_ROWS, 128), jnp.float32),
            pltpu.VMEM((tiles, PADDED, 128), jnp.float32),
            pltpu.SemaphoreType.DMA((tiles,)),
        ],
    )(codes)


def solution(mesh):
    in_specs = (
        P("orb", None, None, "box"),
        P("orb", None, None, "box"),
        P("orb", "box"),
        P("box"),
        P("box"),
        P("box"),
    )
    out_specs = P(None, "box")
    return jax.shard_map(shards, mesh=mesh, in_specs=in_specs, out_specs=out_specs, check_vma=False)
```

```python
import math

import jax
import jax.numpy as jnp
import numpy as np
from jax import lax
from jax.experimental import pallas as pl
from jax.experimental.pallas import tpu as pltpu
from jax.sharding import PartitionSpec as P

SPILL = 32


def legendre_pair(order, where):
    before = where * 0.0 + 1.0
    value = where
    for degree in range(1, order):
        before, value = (value, ((2 * degree + 1) * where * value - degree * before) / (degree + 1))
    return (value, before)


def gauss_rule(order):
    nodes = np.cos(np.pi * (np.arange(order) + 0.75) / (order + 0.5))
    for repeat in range(40):
        value, before = legendre_pair(order, nodes)
        slope = order * (nodes * value - before) / (nodes * nodes - 1.0)
        nodes = nodes - value / slope
    value, before = legendre_pair(order, nodes)
    slope = order * (nodes * value - before) / (nodes * nodes - 1.0)
    weights = 2.0 / ((1.0 - nodes * nodes) * slope * slope)
    return (nodes[::-1], weights[::-1])


def legendre_basis(where):
    shifted = 2.0 * where - 1.0
    rows = [shifted * 0.0 + 1.0, shifted]
    for degree in range(1, 8):
        rows.append(
            ((2 * degree + 1) * shifted * rows[degree] - degree * rows[degree - 1]) / (degree + 1)
        )
    scale = np.sqrt(2.0 * np.arange(9) + 1.0)[:, None]
    return np.stack(rows, 0) * scale


def complement_rows(scaling_rows):
    members = [scaling_rows[index] for index in range(9)]
    kept = []
    identity = np.eye(18)
    for column in range(18):
        vector = identity[column]
        for passes in range(2):
            for member in members + kept:
                vector = vector - np.dot(member, vector) * member
        length = np.sqrt(np.dot(vector, vector))
        if length > 0.1 and len(kept) < 9:
            kept.append(vector / length)
    return np.stack(kept, 0)


def wavelet_tables():
    nodes, weights = gauss_rule(24)
    points = 0.5 * (nodes + 1.0)
    halves = 0.5 * weights
    lower = legendre_basis(0.5 * points) * halves @ legendre_basis(points).T / math.sqrt(2.0)
    upper = legendre_basis(0.5 * points + 0.5) * halves @ legendre_basis(points).T / math.sqrt(2.0)
    scaling_rows = np.concatenate([lower, upper], 1)
    wavelet_rows = complement_rows(scaling_rows)
    matrix = np.concatenate([scaling_rows, wavelet_rows], 0).reshape(2, 9, 2, 9)
    gauss, gauss_weights = gauss_rule(9)
    quad = legendre_basis(0.5 * (gauss + 1.0)).T * np.sqrt(0.5 * gauss_weights)[:, None]
    return (matrix.reshape(18, 2, 9), quad)


ROWS = 729
PADDED = 800
SEGMENT = 92
HALVES = (((0, 1), (2, 3, 4)), ((5, 6), (7, 8), (9, 10)))
GROUPS = ((0, 1), (2, 3), (4, 5), (6, 7), (8, 9, 10))
THIRD_GROUPS = ((0, 1), (2, 3))
QUARTER = 192
PARTS = 3
WIDTH = 27
PIECE = 243
PIECE_ROWS = 256
CUTS = (0, 5, 9)
SPLITS = ((0, 144), (144, 256))
PART_ROWS = 288
LAG = 2


def local_keys(keys, boxes):
    key = keys - lax.axis_index("box") * (8 * boxes)
    return (lax.shift_right_arithmetic(key, 3), key & 7)


def spread_matrix(boxes, group):
    source = lax.broadcasted_iota(jnp.int32, (boxes, 128), 0)
    target = lax.broadcasted_iota(jnp.int32, (boxes, 128), 1)
    hit = (source - (boxes - SPILL) == target - SPILL * group) & (source >= boxes - SPILL)
    return hit.astype(jnp.float32).astype(jnp.bfloat16)


def pick_own(column, boxes):
    row = lax.broadcasted_iota(jnp.int32, (boxes, column.shape[1]), 0)
    return (row == column).astype(jnp.float32)


def pick_spilled(column, group):
    row = lax.broadcasted_iota(jnp.int32, (128, column.shape[1]), 0)
    hit = (row == column + SPILL * (group + 1)) & (column < 0)
    return hit.astype(jnp.float32)


def fill_coefficients(coef_ref, octant, table):
    for axis in range(3):
        bit = jnp.broadcast_to((octant >> axis) & 1, (8, 128)) == 1
        for k in range(18):
            for f in range(9):
                coef_ref[axis * 162 + k * 9 + f] = jnp.where(
                    bit, np.float32(table[k, 1, f]), np.float32(table[k, 0, f])
                )


def contract(source_ref, low, high, coef_ref, axis, store, groups=GROUPS, first=0, outputs=9, width=81):
    def load(block, row):
        if len(source_ref.shape) == 2:
            return source_ref[pl.ds(8 * row + block, 8, stride=72), :]
        return source_ref[block, pl.ds(row, 8, stride=9), :]

    for group in groups:
        inputs = [[load(block, l + 72 * t) for block in (low, high) for l in range(9)] for t in group]
        for f in range(outputs):
            sums = [None] * len(group)
            for k in range(18):
                weight = coef_ref[axis * 162 + k * 9 + first + f]
                for n in range(len(group)):
                    term = weight * inputs[n][k]
                    sums[n] = term if sums[n] is None else sums[n] + term
            for n, t in enumerate(group):
                store(width * f + 8 * t, min(8, width - 8 * t), sums[n])


def lower_axis(source_ref, target_ref, coef_ref, axis, start, stop, groups=GROUPS, **kinds):
    def step(index, carry):
        def store(row, count, value):
            target_ref[index, row : row + count, :] = value[:count]

        contract(source_ref, 2 * index, 2 * index + 1, coef_ref, axis, store, groups, **kinds)
        return carry

    lax.fori_loop(start, stop, step, 0)


def dot(left, right):
    return jnp.dot(left, right, preferred_element_type=jnp.float32)


def scale_of(steps):
    return jnp.exp2(steps * np.float32(1.0 / 256.0))


def encode(value):
    rows = value.shape[0]
    last = lax.broadcasted_iota(jnp.int32, (8, 128), 0) == 7
    top = jnp.maximum(jnp.max(jnp.abs(value), axis=0, keepdims=True), 1e-30)
    steps = jnp.ceil(jnp.log2(top) * 256.0)
    code = jnp.round(value * (32700.0 / scale_of(steps)))
    code = jnp.concatenate([code[: rows - 8], jnp.where(last, steps, code[rows - 8 :])], 0)
    return code.astype(jnp.int32).astype(jnp.int16)


def decode_square(code):
    rows = code.shape[0]
    last = lax.broadcasted_iota(jnp.int32, (8, 128), 0) == 7
    code = code.astype(jnp.int32).astype(jnp.float32)
    value = code * (scale_of(code[rows - 1 : rows]) * np.float32(1.0 / 32700.0))
    value = jnp.concatenate([value[: rows - 8], jnp.where(last, 0.0, value[rows - 8 :])], 0)
    return value * value


def spread_row(row):
    for (start, stop), first, after in zip(SPLITS, CUTS, CUTS[1:]):
        if row < after * WIDTH:
            return row - first * WIDTH + start


def density_kernel(
    counts_hbm, coarse_hbm, waves_hbm, flags_hbm, key1_hbm, key2_hbm, out_hbm,
    counts_ref, flags_ref, key1_ref, key2_ref, sum_code, coarse_ref, waves_ref, coarse_pack_ref, coarse_halo_ref, pack_ref, halo_ref, level_ref, fine_ref, spill_ref, spilled_ref,
    x_ref, a_ref, b_ref, part_a_ref, part_b_ref, coef_ref, value_ref, code_ref, got_outer, got_middle,
    load_sem, small_sem, out_sem, halo_send, halo_recv, code_send, outer_recv, middle_recv, sum_send, sum_recv, *, count, ranges, table, valued
):
    boxes = coarse_hbm.shape[-1]
    pieces = code_ref.shape[0]
    tiles = pieces // PARTS
    me, position = lax.axis_index("orb"), lax.axis_index("box")
    after, before = lax.rem(position + 1, ranges), lax.rem(position + ranges - 1, ranges)
    half = count // 2
    inward = jnp.where(me < half, me + 1, me - 1)
    outward = jnp.where(me < half, me - 1, me + 1)
    outermost = (me == 0) | (me == count - 1)
    middle = (me == half - 1) | (me == half)
    first_range, last_range = position == 0, position == ranges - 1
    mesh_id = pl.DeviceIdType.MESH
    load_coarse = []
    for h in range(2):
        rows_in = pl.ds(4 * SEGMENT * h, min(4 * SEGMENT, ROWS - 4 * SEGMENT * h))
        load_coarse.append(pltpu.make_async_copy(coarse_hbm.at[rows_in], coarse_ref.at[rows_in], load_sem.at[h]))
    load_waves = pltpu.make_async_copy(waves_hbm, waves_ref, load_sem.at[2])
    for copy in (*load_coarse, load_waves):
        copy.start()
    small = [
        pltpu.make_async_copy(source, target, small_sem.at[n])
        for n, (source, target) in enumerate(
            ((counts_hbm, counts_ref), (flags_hbm, flags_ref), (key1_hbm, key1_ref), (key2_hbm, key2_ref))
        )
    ]
    for copy in small:
        copy.start()
    barrier = pltpu.get_barrier_semaphore()
    pl.semaphore_signal(barrier, inc=1, device_id={"orb": inward}, device_id_type=mesh_id)

    @pl.when(jnp.logical_not(outermost))
    def greet_outward():
        pl.semaphore_signal(barrier, inc=1, device_id={"orb": outward}, device_id_type=mesh_id)

    @pl.when(jnp.logical_not(first_range))
    def greet_before():
        pl.semaphore_signal(barrier, inc=1, device_id={"box": before}, device_id_type=mesh_id)

    def remote(source, target, sends, recvs, device):
        return pltpu.make_async_remote_copy(
            src_ref=source,
            dst_ref=target,
            send_sem=sends,
            recv_sem=recvs,
            device_id=device,
            device_id_type=mesh_id,
        )

    def halo(source, target, index):
        return remote(source, target, halo_send.at[index], halo_recv.at[index], {"box": after})

    def part_of(ref, n, s):
        return ref.at[n, pl.ds(SPLITS[s][0], SPLITS[s][1] - SPLITS[s][0])]

    def inner_copy(slots, recvs, n, s):
        return remote(part_of(code_ref, n, s), part_of(slots, n, s), code_send.at[n, s], recvs.at[n, s], {"orb": inward})

    def to_outer_slot(n, s):
        return inner_copy(got_outer, outer_recv, n, s)

    def to_middle_slot(n, s):
        return inner_copy(got_middle, middle_recv, n, s)

    def to_total(n, s):
        part = part_of(sum_code, n, s)
        return remote(part, part, sum_send.at[n, s], sum_recv.at[n, s], {"orb": outward})

    def put_out(n, s):
        return pltpu.make_async_copy(part_of(sum_code, n, s), part_of(out_hbm, n, s), out_sem.at[n, s])

    def when_not(condition):
        return pl.when(jnp.logical_not(condition))

    def send_halo(copy):
        @when_not(last_range)
        def send():
            copy.start()

    def wait_halo(copy):
        @when_not(first_range)
        def wait():
            copy.wait_recv()

    def send_partial(n, s, value):
        start, stop = SPLITS[s]
        code_ref[n, start:stop] = encode(value)

        @pl.when(middle)
        def exchange():
            to_middle_slot(n, s).start()

        @when_not(middle)
        def pass_in():
            to_outer_slot(n, s).start()

    def combine(n):
        @when_not(outermost)
        def add():
            for s, (start, stop) in enumerate(SPLITS):
                to_outer_slot(n, s).wait_recv()
                own = value_ref[n, start:stop]
                send_partial(n, s, jnp.sqrt(decode_square(got_outer[n, start:stop]) + own * own))

    def finish(n):
        for s, (start, stop) in enumerate(SPLITS):

            @pl.when(middle)
            def close():
                to_middle_slot(n, s).wait_recv()
                total = decode_square(code_ref[n, start:stop]) + decode_square(got_middle[n, start:stop])
                sum_code[n, start:stop] = encode(jnp.sqrt(2.0 * total))

            @when_not(middle | outermost)
            def receive():
                to_total(n, s).wait_recv()

            @when_not(outermost)
            def pass_out():
                to_total(n, s).start()

    coarse_halo = [halo(coarse_pack_ref.at[h], coarse_halo_ref.at[h], h) for h in range(2)]
    waves_halo = halo(pack_ref, halo_ref, 2)
    fine_halo = halo(spill_ref, spilled_ref, 3)

    @pl.when(first_range)
    def no_halo():
        for ref in (coarse_halo_ref, halo_ref, spilled_ref):
            ref[...] = jnp.zeros(ref.shape, ref.dtype)

    spread = [spread_matrix(boxes, g) for g in range(4)]
    tail = 8 * SEGMENT - ROWS
    coarse_ref[ROWS : ROWS + tail] = jnp.zeros((tail, 8, boxes), jnp.bfloat16)

    def segment(index):
        return coarse_ref[SEGMENT * index : SEGMENT * (index + 1)].reshape(8 * SEGMENT, boxes)

    for h in range(2):
        load_coarse[h].wait()
        total = dot(segment(4 * h), spread[0])
        for g in range(1, 4):
            total = total + dot(segment(4 * h + g), spread[g])
        coarse_pack_ref[h] = total.astype(jnp.bfloat16)
        if h == 0:
            pl.semaphore_wait(barrier, 1 + jnp.where(outermost, 0, 1) + jnp.where(last_range, 0, 1))
        send_halo(coarse_halo[h])
    load_waves.wait()
    for copy in small:
        copy.wait()
    keep = jnp.broadcast_to((1 - flags_ref[...]).astype(jnp.float32), (16, boxes)).astype(jnp.bfloat16)
    packed_keep = sum(dot(keep, s) for s in spread)[:1]
    for h in range(2):
        total = None
        for g in range(4):
            if 4 * h + g > 0:
                term = dot(waves_ref[0, 4 * h + g - 1], spread[g])
                total = term if total is None else total + term
        pack_ref[h] = (total * packed_keep).astype(jnp.bfloat16)
    send_halo(waves_halo)
    column, octant = local_keys(key1_ref[...], boxes)
    fill_coefficients(coef_ref.at[tiles], octant, table)
    own = pick_own(column, boxes)
    fine_ref[ROWS - 1 : 4 * QUARTER, :] = jnp.zeros((4 * QUARTER - ROWS + 1, 128), jnp.float32)
    for (start, stop), first, after in zip(SPLITS, CUTS, CUTS[1:]):
        start = (start + (after - first) * WIDTH) // 8 * 8
        value_ref[:, start:stop, :] = jnp.zeros((pieces, stop - start, 128), jnp.float32)

    def leaf_coefficients(t, carry):
        fill_coefficients(coef_ref.at[t], local_keys(key2_ref[t], boxes)[1], valued)
        return carry

    lax.fori_loop(0, tiles, leaf_coefficients, 0)
    coef = coef_ref.at[tiles]
    for h in range(2):
        wait_halo(coarse_halo[h])
        for g in range(4):
            pick = jnp.concatenate([own, pick_spilled(column, g)], 0).astype(jnp.bfloat16)
            both = jnp.concatenate([segment(4 * h + g), coarse_halo_ref[h]], 1)
            start = 8 * SEGMENT * (4 * h + g)
            level_ref[start : start + 8 * SEGMENT, :] = dot(both, pick)
        lower_axis(level_ref, a_ref, coef, 0, 0, 4, HALVES[h])
    lower_axis(a_ref, b_ref, coef, 1, 0, 2)

    def store_fine(row, rows_in, value):
        fine_ref[row : row + rows_in, :] = value[:rows_in]

    contract(b_ref, 0, 1, coef, 2, store_fine)
    for part in range(2):
        total = None
        for g in range(4):
            quarter = fine_ref[QUARTER * g : QUARTER * (g + 1), :]
            half_value = quarter.astype(jnp.bfloat16)
            if part == 1:
                half_value = (quarter - half_value.astype(jnp.float32)).astype(jnp.bfloat16)
            term = dot(half_value, spread[g])
            total = term if total is None else total + term
        spill_ref[part] = total.astype(jnp.bfloat16)
    send_halo(fine_halo)

    columns = jnp.concatenate([local_keys(key2_ref[t], boxes)[0] for t in range(tiles)], 1)
    own = pick_own(columns, boxes)
    own_kept = own * dot(keep, own.astype(jnp.bfloat16))[:1]

    def store_blocks(block, start, rows_in, value):
        for t in range(tiles):
            x_ref[t, block, start : start + rows_in, :] = value[:, 128 * t : 128 * (t + 1)]

    wait_halo(waves_halo)
    for g in range(4):
        pick = jnp.concatenate([own_kept, pick_spilled(columns, g)], 0).astype(jnp.bfloat16)
        for h in range(2):
            if 4 * h + g > 0:
                both = jnp.concatenate([waves_ref[0, 4 * h + g - 1], halo_ref[h]], 1)
                store_blocks(4 * h + g, 0, ROWS, dot(both, pick))

    def leaf_axis(t, part, start, stop):
        lower_axis(
            x_ref.at[t], part_a_ref.at[part], coef_ref.at[t], 0, start, stop, first=3 * part, outputs=3
        )

    for part in range(PARTS):
        leaf_axis(0, part, 1, 4)
    wait_halo(fine_halo)
    for g in range(4):
        pick = jnp.concatenate([own, pick_spilled(columns, g)], 0).astype(jnp.bfloat16)
        quarter = fine_ref[QUARTER * g : QUARTER * (g + 1), :]
        high = quarter.astype(jnp.bfloat16)
        low = (quarter - high.astype(jnp.float32)).astype(jnp.bfloat16)
        total = dot(jnp.concatenate([high, spilled_ref[0]], 1), pick)
        total = total + dot(jnp.concatenate([low, spilled_ref[1]], 1), pick)
        store_blocks(0, QUARTER * g, QUARTER, total)
    for n in range(pieces):
        t, part = n // PARTS, n % PARTS
        leaf_axis(t, part, 0, 1 if t == 0 else 4)
        kinds = dict(groups=THIRD_GROUPS, width=WIDTH)
        lower_axis(part_a_ref.at[part], part_b_ref, coef_ref.at[t], 1, 0, 2, **kinds)
        slot = t * 128 + lax.broadcasted_iota(jnp.int32, (8, 128), 1)
        live = jnp.where(slot < counts_ref[0], 1.0, 0.0).astype(jnp.float32)

        def store_value(row, rows_in, value):
            row = spread_row(row)
            value_ref[n, row : row + rows_in, :] = (value * live)[:rows_in]

        contract(part_b_ref, 0, 1, coef_ref.at[t], 2, store_value, **kinds)

        @pl.when(outermost)
        def start_chain():
            for s, (start, stop) in enumerate(SPLITS):
                send_partial(n, s, value_ref[n, start:stop])

        if n >= LAG:
            combine(n - LAG)
        if n >= 2 * LAG:
            finish(n - 2 * LAG)
    for n in range(pieces, pieces + 2 * LAG):
        if 0 <= n - LAG < pieces:
            combine(n - LAG)
        if 0 <= n - 2 * LAG:
            finish(n - 2 * LAG)

    every = [(n, s) for n in range(pieces) for s in range(len(SPLITS))]
    for n, s in every:

        @pl.when(outermost & jnp.logical_not(middle))
        def totals_received():
            to_total(n, s).wait_recv()

        put_out(n, s).start()

    @when_not(last_range)
    def halos_sent():
        for copy in (*coarse_halo, waves_halo, fine_halo):
            copy.wait_send()

    for n, s in every:
        to_outer_slot(n, s).wait_send()

        @when_not(outermost)
        def totals_sent():
            to_total(n, s).wait_send()

        put_out(n, s).wait()


def decode_kernel(code_hbm, out_hbm, code_ref, piece_ref, value_ref, in_sem, sem):
    pieces = code_ref.shape[0]
    tiles = pieces // PARTS
    loads = [pltpu.make_async_copy(code_hbm.at[n], code_ref.at[n], in_sem.at[n]) for n in range(pieces)]
    for copy in loads:
        copy.start()

    def out_copy(t):
        return pltpu.make_async_copy(
            value_ref.at[t, pl.ds(0, ROWS)], out_hbm.at[:, pl.ds(128 * t, 128)], sem.at[t]
        )

    for n in range(pieces):
        t, part = n // PARTS, n % PARTS
        loads[n].wait()
        for start, stop in SPLITS:
            piece_ref[n, start:stop, :] = decode_square(code_ref[n, start:stop])
        for f in range(3):
            for first, after in zip(CUTS, CUTS[1:]):
                for k in range(9 * first, 9 * after, 8):
                    rows = min(8, 9 * after - k)
                    value = piece_ref[n, pl.ds(spread_row(3 * k + f), rows, stride=3), :]
                    value_ref[t, pl.ds(9 * k + 3 * part + f, rows, stride=9), :] = value
        if part == PARTS - 1:
            out_copy(t).start()
    for t in range(tiles):
        out_copy(t).wait()


def shards(coarse, wavelets, leaf_flags, child_key1, child_key2, counts):
    matrix, quad = wavelet_tables()
    valued = np.einsum("kop,gp->kog", matrix, quad)
    boxes = coarse.shape[-1]
    slots = child_key2.shape[0]
    count, ranges = lax.axis_size("orb"), lax.axis_size("box")
    tiles = slots // 128
    pieces = PARTS * tiles
    anywhere = pl.BlockSpec(memory_space=pltpu.HBM)
    codes = pl.pallas_call(
        lambda *refs: density_kernel(*refs, count=count, ranges=ranges, table=matrix, valued=valued),
        out_shape=jax.ShapeDtypeStruct((pieces, PIECE_ROWS, 128), jnp.int16),
        in_specs=[anywhere] * 6,
        out_specs=anywhere,
        scratch_shapes=[
            pltpu.SMEM((1,), jnp.int32),
            pltpu.VMEM((1, boxes), jnp.int32),
            pltpu.VMEM((1, boxes), jnp.int32),
            pltpu.VMEM((tiles, 1, 128), jnp.int32),
            pltpu.VMEM((pieces, PIECE_ROWS, 128), jnp.int16),
            pltpu.VMEM((8 * SEGMENT, 8, boxes), jnp.bfloat16),
            pltpu.VMEM(wavelets.shape, jnp.bfloat16),
            pltpu.VMEM((2, 8 * SEGMENT, 128), jnp.bfloat16),
            pltpu.VMEM((2, 8 * SEGMENT, 128), jnp.bfloat16),
            pltpu.VMEM((2, ROWS, 128), jnp.bfloat16),
            pltpu.VMEM((2, ROWS, 128), jnp.bfloat16),
            pltpu.VMEM((8 * PADDED, 128), jnp.float32),
            pltpu.VMEM((4 * QUARTER, 128), jnp.float32),
            pltpu.VMEM((2, QUARTER, 128), jnp.bfloat16),
            pltpu.VMEM((2, QUARTER, 128), jnp.bfloat16),
            pltpu.VMEM((tiles, 8, PADDED, 128), jnp.float32),
            pltpu.VMEM((4, PADDED, 128), jnp.float32),
            pltpu.VMEM((2, PADDED, 128), jnp.float32),
            pltpu.VMEM((PARTS, 4, PART_ROWS, 128), jnp.float32),
            pltpu.VMEM((2, PART_ROWS, 128), jnp.float32),
            pltpu.VMEM((tiles + 1, 3 * 162, 8, 128), jnp.float32),
            pltpu.VMEM((pieces, PIECE_ROWS, 128), jnp.float32),
            pltpu.VMEM((pieces, PIECE_ROWS, 128), jnp.int16),
            pltpu.VMEM((pieces, PIECE_ROWS, 128), jnp.int16),
            pltpu.VMEM((pieces, PIECE_ROWS, 128), jnp.int16),
            pltpu.SemaphoreType.DMA((3,)),
            pltpu.SemaphoreType.DMA((4,)),
            pltpu.SemaphoreType.DMA((pieces, len(SPLITS))),
            pltpu.SemaphoreType.DMA((4,)),
            pltpu.SemaphoreType.DMA((4,)),
        ]
        + [pltpu.SemaphoreType.DMA((pieces, len(SPLITS)))] * 5,
        compiler_params=pltpu.CompilerParams(
            collective_id=0, has_side_effects=True, vmem_limit_bytes=60 * 1024 * 1024
        ),
    )(
        counts,
        jnp.transpose(coarse[0], (1, 0, 2)),
        wavelets,
        leaf_flags,
        child_key1.reshape(1, boxes),
        child_key2.reshape(tiles, 1, 128),
    )
    return pl.pallas_call(
        decode_kernel,
        out_shape=jax.ShapeDtypeStruct((ROWS, slots), jnp.float32),
        in_specs=[anywhere],
        out_specs=anywhere,
        scratch_shapes=[
            pltpu.VMEM((pieces, PIECE_ROWS, 128), jnp.int16),
            pltpu.VMEM((pieces, PIECE_ROWS, 128), jnp.float32),
            pltpu.VMEM((tiles, PADDED, 128), jnp.float32),
            pltpu.SemaphoreType.DMA((pieces,)),
            pltpu.SemaphoreType.DMA((tiles,)),
        ],
    )(codes)


def solution(mesh):
    in_specs = (
        P("orb", None, None, "box"),
        P("orb", None, None, "box"),
        P("orb", "box"),
        P("box"),
        P("box"),
        P("box"),
    )
    out_specs = P(None, "box")
    return jax.shard_map(shards, mesh=mesh, in_specs=in_specs, out_specs=out_specs, check_vma=False)
```
